32 devices in a mesh: row: 4 (over y, core), col: 8 (over z, x).
Axes of the slice: x: 2, y: 2, z: 4, core: 2. Of those that a mesh axis runs over, the one named last changes fastest.
Arguments:
- elem_residual: bfloat16 [16384, 3, 256], P(('row', 'col')), may hold values from -6 to 6
- corners: int32 [16384, 3], P(('row', 'col')), may hold values from 0 to 383
- share_rows: int32 [32, 2, 64], P(('row', 'col')), may hold values from 0 to 255
- x_factor: bfloat16 [8192, 1728], P(('row', 'col')), may hold values from -0.40039062 to 0.40039062, as said below
Outputs:
- solution: float32 [8192, 256], P(('row', 'col'))
The draws below stay inside these ranges and needn't reach their ends.
Inputs may be any that keep to these rules, and one draw needn't show every extreme that they name: `corners`: values below 256 are own vertices, the next 64 the slots shared with the left neighbour, the last 64 those shared with the right neighbour. `share_rows`: own row indices; a row may appear several times. `x_factor`: independent entries, each column block with its own scale.
All inputs are finite; a program needn't handle non-finite values.
Results may differ from the reference program's by a relative error of at most 0.0035.
Values sent between devices are 32-bit elements; how exact they have to be, the bound alone decides.
A program may use at most 64 MiB of HBM per device.

```python
import jax
import jax.numpy as jnp
from jax import lax

RHS = 256
ROWS_DEV = 256
ELEMS = 512
SHARED = 64
INNER = 1408
SEP_COLS = 64
LEVELS = 5
COLS = 1728
ROWS = 8192
N_ROW = 4
N_COL = 8
DEVICES = 32


def draw_x_factor(key, part):
    columns = jnp.arange(COLS, dtype=jnp.int32)
    level = jnp.maximum(columns - INNER, 0) // SEP_COLS + 1
    level_scale = (jnp.exp2(level.astype(jnp.float32)) * ROWS_DEV * SEP_COLS) ** (-0.25)
    inner_scale = jnp.float32(ROWS_DEV * INNER) ** (-0.25)
    scales = jnp.where(columns < INNER, inner_scale, level_scale)
    entries = jnp.clip(jax.random.normal(jax.random.fold_in(key, 7), (ROWS, COLS), jnp.float32), -5.3, 5.3)
    return jnp.clip(entries * scales[None, :], -0.4, 0.4).astype(jnp.bfloat16)


def plant(array, stream_key, low, top_value):
    dims = array.shape
    index_at = [jax.random.randint(jax.random.fold_in(stream_key, axis), (), 0, dims[axis]) for axis in range(len(dims))]
    array = array.at[tuple(index_at)].set(low)
    longest = dims.index(max(dims))
    index_at[longest] = (index_at[longest] + 1) % dims[longest]
    return array.at[tuple(index_at)].set(top_value)


def block_levels(rng, shape, pieces, smallest, high):
    level, own = 1.0, jax.random.fold_in(rng, 6)
    for dim, parts in pieces:
        heights = jnp.exp(jax.random.uniform(jax.random.fold_in(own, dim), (parts,), jnp.float32, smallest / len(pieces), high / len(pieces)))
        level = level * jnp.repeat(heights, shape[dim] // parts).reshape([-1 if axis == dim else 1 for axis in range(len(shape))])
    return level


def centred(rng, shape, deviation, reach, pieces=(), kind=jnp.bfloat16):
    drawn = jax.random.normal(rng, shape, jnp.float32) * deviation
    if len(pieces) > 0:
        drawn = block_levels(rng, shape, pieces, -0.22, 0.18) * drawn
    return jnp.clip(drawn, min=-reach, max=reach).astype(kind)


def setup_inputs(seed: int = 0) -> dict:
    keys = jax.random.split(jax.random.key(seed), 5)
    return {
        "elem_residual": centred(keys[0], (DEVICES * ELEMS, 3, RHS), 1.0, 6.0, ((0, 32),)),
        "corners": plant(jax.random.randint(keys[1], (DEVICES * ELEMS, 3), 0, ROWS_DEV + 2 * SHARED), jax.random.fold_in(keys[1], 1), 0, (ROWS_DEV + 2 * SHARED) - 1).astype(jnp.int32),
        "share_rows": plant(jax.random.randint(keys[2], (DEVICES, 2, SHARED), 0, ROWS_DEV), jax.random.fold_in(keys[2], 1), 0, ROWS_DEV - 1).astype(jnp.int32),
        "x_factor": draw_x_factor(jax.random.fold_in(keys[4], 71), 0),
    }


def reference(elem_residual, corners, share_rows, x_factor):
    count = N_ROW * N_COL
    ext_len = ROWS_DEV + 2 * SHARED
    offsets = jnp.arange(count, dtype=jnp.int32)
    ids = corners.reshape(count, ELEMS * 3) + (offsets * ext_len)[:, None]
    values = elem_residual.astype(jnp.float32).reshape(count * ELEMS * 3, RHS)
    extended = jax.ops.segment_sum(values, ids.reshape(-1), num_segments=count * ext_len)
    extended = extended.reshape(N_ROW, N_COL, ext_len, RHS)
    owned = extended[:, :, :ROWS_DEV].reshape(count * ROWS_DEV, RHS)
    to_left = extended[:, :, ROWS_DEV:ROWS_DEV + SHARED]
    to_right = extended[:, :, ROWS_DEV + SHARED:]
    from_left = jnp.roll(to_right, 1, axis=1)
    from_right = jnp.roll(to_left, -1, axis=1)
    received = jnp.concatenate([from_left, from_right], axis=2).reshape(count * 2 * SHARED, RHS)
    targets = (share_rows.reshape(count, 2 * SHARED) + (offsets * ROWS_DEV)[:, None]).reshape(-1)
    assembled = owned + jax.ops.segment_sum(received, targets, num_segments=count * ROWS_DEV)
    rhs_local = assembled.astype(jnp.bfloat16).reshape(count, ROWS_DEV, RHS)
    factor = x_factor.reshape(count, ROWS_DEV, COLS)

    def inner_part(pair):
        block, local = pair
        inner = block[:, :INNER]
        weights = jnp.dot(inner.T, local, preferred_element_type=jnp.float32).astype(jnp.bfloat16)
        return jnp.dot(inner, weights, preferred_element_type=jnp.float32)

    solution = lax.map(inner_part, (factor, rhs_local))

    def separator_part(pair):
        block, local = pair
        return jnp.dot(block[:, INNER:].T, local, preferred_element_type=jnp.float32)

    partial_value = lax.map(separator_part, (factor, rhs_local)).reshape(count, LEVELS, SEP_COLS, RHS)
    summed = []
    for level in range(LEVELS):
        group = 2 ** (level + 1)
        totals = partial_value[:, level].reshape(count // group, group, SEP_COLS, RHS).sum(axis=1)
        summed.append(jnp.repeat(totals, group, axis=0).astype(jnp.bfloat16))
    coef = jnp.stack(summed, axis=1).reshape(count, LEVELS * SEP_COLS, RHS)

    def apply_part(pair):
        block, weights = pair
        return jnp.dot(block[:, INNER:], weights, preferred_element_type=jnp.float32)

    solution = solution + lax.map(apply_part, (factor, coef))
    return solution.reshape(count * ROWS_DEV, RHS)
```

```python
import functools

import jax
import jax.numpy as jnp
from jax import lax
from jax.experimental import pallas as pl
from jax.experimental.pallas import tpu as pltpu
from jax.sharding import PartitionSpec as P

INNER = 1408
MESH = pl.DeviceIdType.MESH
F32 = jnp.float32
BF16 = jnp.bfloat16


def swapped(block, axis, stride):
    count = lax.axis_size(axis)
    route = []
    for low in range(count):
        high = low | 1 << stride
        if high != low and high < count:
            route += [(low, high), (high, low)]
    return lax.ppermute(block, axis, route)


def summed_levels(blocks, n_row, n_col):
    col_bits = n_col.bit_length() - 1
    row_bits = n_row.bit_length() - 1
    for bit in range(col_bits + row_bits):
        axis, stride = ("col", bit) if bit < col_bits else ("row", bit - col_bits)
        partner = swapped(blocks[bit:], axis, stride)
        blocks = jnp.concatenate([blocks[:bit], blocks[bit:] + partner], axis=0)
    return blocks


def by_rounds(n_row, n_col, elem_residual, corners, share_rows, x_factor):
    rows_dev = x_factor.shape[0]
    shared = share_rows.shape[2]
    width = elem_residual.shape[2]
    levels = (n_row * n_col).bit_length() - 1
    ext_len = rows_dev + 2 * shared
    flat_ids = corners.reshape(-1)
    onehot = (
        lax.broadcasted_iota(jnp.int32, (ext_len, flat_ids.shape[0]), 0) == flat_ids[None, :]
    ).astype(BF16)
    extended = jnp.dot(onehot, elem_residual.reshape(-1, width), preferred_element_type=F32)
    forward = [(i, (i + 1) % n_col) for i in range(n_col)]
    backward = [(target, source) for source, target in forward]
    from_left = lax.ppermute(extended[rows_dev + shared :], "col", forward)
    from_right = lax.ppermute(extended[rows_dev : rows_dev + shared], "col", backward)
    row_ids = lax.broadcasted_iota(jnp.int32, (rows_dev, shared), 0)
    assembled = extended[:rows_dev]
    for side, received in ((0, from_left), (1, from_right)):
        side_map = (row_ids == share_rows[0, side][None, :]).astype(F32)
        assembled = assembled + jnp.dot(
            side_map, received, precision=lax.Precision.HIGHEST, preferred_element_type=F32
        )
    partial_value = lax.dot_general(
        x_factor, assembled.astype(BF16), (((0,), (0,)), ((), ())), preferred_element_type=F32
    )
    blocks = partial_value[INNER:].reshape(levels, -1, width)
    blocks = summed_levels(blocks, n_row, n_col)
    coef = jnp.concatenate([partial_value[:INNER], blocks.reshape(-1, width)], axis=0)
    return jnp.dot(x_factor, coef.astype(BF16), preferred_element_type=F32)


class Plan:
    def __init__(self, n_row, n_col, sep):
        self.n_row, self.n_col, self.sep = n_row, n_col, sep
        self.n_z = n_col // 2
        self.levels = (n_row * n_col).bit_length() - 1

    def z_span(self, level):
        return min(2 ** (level - 1), self.n_z)

    def row_span(self, level):
        return max(1, 2**level // self.n_col)

    def piece(self, level):
        return self.sep // self.z_span(level)


def takes(n_row, n_col, sep):
    return n_col >= 4 and n_row <= 4 and sep % (8 * (n_col // 2)) == 0


def tdot(a, b):
    return lax.dot_general(a, b, (((0,), (0,)), ((), ())), preferred_element_type=F32)


def kernel(
    plan,
    er_hbm, cor_hbm, sh_hbm, x_hbm,
    out_ref,
    er, cor, sh, xt,
    halo_out, halo_in, own, rhs, part, l1_in, rs_in, ex_out, ex_in, final,
    in_sem, halo_s, halo_r, l1_s, l1_r, rs_s, rs_r, ex_s, ex_r, ag_s, ag_r,
):
    row, col = lax.axis_index("row"), lax.axis_index("col")
    z, x = col // 2, col % 2
    levels, n_col = plan.levels, plan.n_col
    rows_dev = out_ref.shape[0]
    shared = halo_out.shape[1]
    kinds = er.shape[0]
    elems = er.shape[1]
    inner = xt.shape[0] - plan.sep * levels

    loads = [
        pltpu.make_async_copy(source, target, in_sem.at[i])
        for i, (source, target) in enumerate(
            ((cor_hbm, cor), (er_hbm, er), (sh_hbm, sh), (x_hbm, xt))
        )
    ]
    for load in loads:
        load.start()

    right = (row, (col + 1) % n_col)
    left = (row, (col + n_col - 1) % n_col)

    def z_peer(level, m):
        span = plan.z_span(level)
        local = z % span
        return (row, (z - local + (local + m) % span) * 2 + x)

    def side_peer(level, a, k):
        span = plan.row_span(level)
        local = row % span
        return (row - local + (local + k) % span, z * 2 + (x + a) % 2)

    top = levels
    greeted = [left, right]
    greeted += [z_peer(top, m) for m in range(1, plan.n_z)]
    greeted += [
        side_peer(top, a, k)
        for a in range(2)
        for k in range(plan.row_span(top))
        if a or k
    ]
    barrier = pltpu.get_barrier_semaphore()
    for peer in greeted:
        pl.semaphore_signal(barrier, inc=1, device_id=peer, device_id_type=MESH)

    def assembled_rows(start, count):
        total = None
        for k in range(kinds):
            ids = cor[k : k + 1, :]
            at = lax.broadcasted_iota(jnp.int32, (count, elems), 0) + start
            onehot = jnp.where(at == ids, 1.0, 0.0).astype(BF16)
            term = jnp.dot(onehot, er[k], preferred_element_type=F32)
            total = term if total is None else total + term
        return total

    loads[0].wait()
    loads[1].wait()
    halo_out[...] = assembled_rows(rows_dev, 2 * shared).reshape(halo_out.shape)
    pl.semaphore_wait(barrier, len(greeted))

    def remote(source, target, send, recv, peer):
        copy = pltpu.make_async_remote_copy(
            src_ref=source,
            dst_ref=target,
            send_sem=send,
            recv_sem=recv,
            device_id=peer,
            device_id_type=MESH,
        )
        copy.start()
        return copy

    sent = []
    halo = [
        remote(halo_out.at[1], halo_in.at[0], halo_s.at[0], halo_r.at[0], right),
        remote(halo_out.at[0], halo_in.at[1], halo_s.at[1], halo_r.at[1], left),
    ]
    sent += halo

    own[...] = assembled_rows(0, rows_dev)
    loads[2].wait()
    targets = jnp.concatenate([sh[0:1, :], sh[1:2, :]], axis=1)
    at = lax.broadcasted_iota(jnp.int32, (rows_dev, 2 * shared), 0)
    share_map = jnp.where(at == targets, 1.0, 0.0).astype(BF16)
    share_map = jnp.concatenate([share_map, share_map], axis=1)
    loads[3].wait()
    for copy in halo:
        copy.wait_recv()
    received = halo_in[...].reshape(2 * shared, -1)
    high = received.astype(BF16)
    low = (received - high.astype(F32)).astype(BF16)
    received = jnp.concatenate([high, low], axis=0)
    assembled = own[...] + jnp.dot(share_map, received, preferred_element_type=F32)
    rhs[...] = assembled.astype(BF16)
    part[...] = jnp.dot(xt[inner:, :], rhs[...], preferred_element_type=F32).reshape(part.shape)

    rs, ex, ag = {}, {}, {}
    order = list(range(levels, 1, -1))
    for level in order:
        span, rows = plan.z_span(level), plan.piece(level)
        for m in range(1, span):
            index = (z % span + m) % span
            rs[level, m] = remote(
                part.at[level - 1, pl.ds(pl.multiple_of(index * rows, 8), rows)],
                rs_in.at[level - 1, m - 1, pl.ds(0, rows)],
                rs_s.at[level - 1, m - 1],
                rs_r.at[level - 1, m - 1],
                z_peer(level, m),
            )
    first = remote(part.at[0], l1_in, l1_s.at[0], l1_r.at[0], side_peer(1, 1, 0))
    sent += list(rs.values()) + [first]

    weights = jnp.dot(xt[:inner, :], rhs[...], preferred_element_type=F32).astype(BF16)
    out_ref[...] = tdot(xt[:inner, :], weights)

    for level in order:
        span, rows = plan.z_span(level), plan.piece(level)
        mine = pl.ds(pl.multiple_of((z % span) * rows, 8), rows)
        total = part[level - 1, mine]
        for m in range(1, span):
            rs[level, m].wait_recv()
            total = total + rs_in[level - 1, m - 1, pl.ds(0, rows)]
        ex_out[level - 1, pl.ds(0, rows)] = total
        r_span = plan.row_span(level)
        for a in range(2):
            for k in range(r_span):
                if a or k:
                    slot = a * r_span + k - 1
                    ex[level, a, k] = remote(
                        ex_out.at[level - 1, pl.ds(0, rows)],
                        ex_in.at[level - 1, slot, pl.ds(0, rows)],
                        ex_s.at[level - 1, slot],
                        ex_r.at[level - 1, slot],
                        side_peer(level, a, k),
                    )
    sent += list(ex.values())
    for level in order:
        span, rows = plan.z_span(level), plan.piece(level)
        mine = pl.ds(pl.multiple_of((z % span) * rows, 8), rows)
        total = ex_out[level - 1, pl.ds(0, rows)]
        r_span = plan.row_span(level)
        for a in range(2):
            for k in range(r_span):
                if a or k:
                    ex[level, a, k].wait_recv()
                    total = total + ex_in[level - 1, a * r_span + k - 1, pl.ds(0, rows)]
        final[level - 1, mine] = total
        for m in range(1, span):
            ag[level, m] = remote(
                final.at[level - 1, mine],
                final.at[level - 1, mine],
                ag_s.at[level - 1, m - 1],
                ag_r.at[level - 1, m - 1],
                z_peer(level, m),
            )
    sent += list(ag.values())
    first.wait_recv()
    final[0] = part[0] + l1_in[...]
    for copy in ag.values():
        copy.wait_recv()
    coef = final[...].reshape(plan.sep * levels, -1).astype(BF16)
    out_ref[...] += tdot(xt[inner:, :], coef)
    for copy in sent:
        copy.wait_send()


def in_one_kernel(plan, elem_residual, corners, share_rows, x_factor):
    rows_dev, cols = x_factor.shape
    shared = share_rows.shape[2]
    elems, kinds, width = elem_residual.shape
    levels, sep = plan.levels, plan.sep
    top = plan.row_span(levels) * 2 - 1
    z_slots = plan.n_z - 1
    half = sep // 2
    dma = pltpu.SemaphoreType.DMA
    anywhere = pl.BlockSpec(memory_space=pl.ANY)
    return pl.pallas_call(
        functools.partial(kernel, plan),
        out_shape=jax.ShapeDtypeStruct((rows_dev, width), F32),
        in_specs=[anywhere] * 4,
        out_specs=pl.BlockSpec(memory_space=pltpu.VMEM),
        scratch_shapes=[
            pltpu.VMEM((kinds, elems, width), BF16),
            pltpu.VMEM((kinds, elems), jnp.int32),
            pltpu.VMEM((2, shared), jnp.int32),
            pltpu.VMEM((cols, rows_dev), BF16),
            pltpu.VMEM((2, shared, width), F32),
            pltpu.VMEM((2, shared, width), F32),
            pltpu.VMEM((rows_dev, width), F32),
            pltpu.VMEM((rows_dev, width), BF16),
            pltpu.VMEM((levels, sep, width), F32),
            pltpu.VMEM((sep, width), F32),
            pltpu.VMEM((levels, z_slots, half, width), F32),
            pltpu.VMEM((levels, half, width), F32),
            pltpu.VMEM((levels, top, half, width), F32),
            pltpu.VMEM((levels, sep, width), F32),
            dma((4,)),
            dma((2,)),
            dma((2,)),
            dma((1,)),
            dma((1,)),
            dma((levels, z_slots)),
            dma((levels, z_slots)),
            dma((levels, top)),
            dma((levels, top)),
            dma((levels, z_slots)),
            dma((levels, z_slots)),
        ],
        compiler_params=pltpu.CompilerParams(collective_id=0, has_side_effects=True),
        name="factor_solve",
    )(
        elem_residual.transpose(1, 0, 2),
        corners.T,
        share_rows.reshape(2, shared),
        x_factor.T,
    )


def solution(mesh):
    n_row, n_col = mesh.shape["row"], mesh.shape["col"]
    levels = (n_row * n_col).bit_length() - 1

    def per_device(elem_residual, corners, share_rows, x_factor):
        sep = (x_factor.shape[1] - INNER) // levels
        args = (elem_residual, corners, share_rows, x_factor)
        if takes(n_row, n_col, sep):
            return in_one_kernel(Plan(n_row, n_col, sep), *args)
        return by_rounds(n_row, n_col, *args)

    placed = (
        P(("row", "col"), None, None),
        P(("row", "col"), None),
        P(("row", "col"), None, None),
        P(("row", "col"), None),
    )
    return jax.shard_map(
        per_device, mesh=mesh, in_specs=placed, out_specs=P(("row", "col"), None), check_vma=False
    )
```

```python
import functools

import jax
import jax.numpy as jnp
from jax import lax
from jax.experimental import pallas as pl
from jax.experimental.pallas import tpu as pltpu
from jax.sharding import PartitionSpec as P

INNER = 1408
MESH = pl.DeviceIdType.MESH
F32 = jnp.float32
BF16 = jnp.bfloat16


def swapped(block, axis, stride):
    count = lax.axis_size(axis)
    route = []
    for low in range(count):
        high = low | 1 << stride
        if high != low and high < count:
            route += [(low, high), (high, low)]
    return lax.ppermute(block, axis, route)


def summed_levels(blocks, n_row, n_col):
    col_bits = n_col.bit_length() - 1
    row_bits = n_row.bit_length() - 1
    for bit in range(col_bits + row_bits):
        axis, stride = ("col", bit) if bit < col_bits else ("row", bit - col_bits)
        partner = swapped(blocks[bit:], axis, stride)
        blocks = jnp.concatenate([blocks[:bit], blocks[bit:] + partner], axis=0)
    return blocks


def by_rounds(n_row, n_col, elem_residual, corners, share_rows, x_factor):
    rows_dev = x_factor.shape[0]
    shared = share_rows.shape[2]
    width = elem_residual.shape[2]
    levels = (n_row * n_col).bit_length() - 1
    ext_len = rows_dev + 2 * shared
    flat_ids = corners.reshape(-1)
    onehot = (
        lax.broadcasted_iota(jnp.int32, (ext_len, flat_ids.shape[0]), 0) == flat_ids[None, :]
    ).astype(BF16)
    extended = jnp.dot(onehot, elem_residual.reshape(-1, width), preferred_element_type=F32)
    forward = [(i, (i + 1) % n_col) for i in range(n_col)]
    backward = [(target, source) for source, target in forward]
    from_left = lax.ppermute(extended[rows_dev + shared :], "col", forward)
    from_right = lax.ppermute(extended[rows_dev : rows_dev + shared], "col", backward)
    row_ids = lax.broadcasted_iota(jnp.int32, (rows_dev, shared), 0)
    assembled = extended[:rows_dev]
    for side, received in ((0, from_left), (1, from_right)):
        side_map = (row_ids == share_rows[0, side][None, :]).astype(F32)
        assembled = assembled + jnp.dot(
            side_map, received, precision=lax.Precision.HIGHEST, preferred_element_type=F32
        )
    partial_value = lax.dot_general(
        x_factor, assembled.astype(BF16), (((0,), (0,)), ((), ())), preferred_element_type=F32
    )
    blocks = partial_value[INNER:].reshape(levels, -1, width)
    blocks = summed_levels(blocks, n_row, n_col)
    coef = jnp.concatenate([partial_value[:INNER], blocks.reshape(-1, width)], axis=0)
    return jnp.dot(x_factor, coef.astype(BF16), preferred_element_type=F32)


class Plan:
    def __init__(self, n_row, n_col, sep):
        self.n_row, self.n_col, self.sep = n_row, n_col, sep
        self.levels = (n_row * n_col).bit_length() - 1
        self.col_bits = n_col.bit_length() - 1
        self.groups = []
        if self.levels > self.col_bits:
            self.groups.append((self.col_bits + 1, self.levels))
        self.groups += [(level, level) for level in range(self.col_bits, 1, -1)]

    def span(self, level):
        return min(2**level, self.n_col)

    def row_span(self, level):
        return max(1, 2**level // self.n_col)

    def piece(self, level):
        return self.sep // self.span(level)


def takes(n_row, n_col, sep):
    return n_col >= 4 and 2 <= n_row <= 4 and sep % (8 * n_col) == 0


def tdot(a, b):
    return lax.dot_general(a, b, (((0,), (0,)), ((), ())), preferred_element_type=F32)


def kernel(
    plan,
    er_hbm, cor_hbm, sh_hbm, x_hbm,
    out_ref,
    er, cor, sh, xt,
    halo_out, halo_in, own, rhs, part, l1_in, rs_in, ex_out, ex_in, final,
    in_sem, halo_s, halo_r, l1_s, l1_r, rs_s, rs_r, ex_s, ex_r, ag_s, ag_r,
):
    row, col = lax.axis_index("row"), lax.axis_index("col")
    levels, n_col = plan.levels, plan.n_col
    rows_dev = out_ref.shape[0]
    shared = halo_out.shape[1]
    kinds = er.shape[0]
    elems = er.shape[1]
    inner = xt.shape[0] - plan.sep * levels

    right = (row, (col + 1) % n_col)
    left = (row, (col + n_col - 1) % n_col)

    def col_peer(span, m):
        local = col % span
        return (row, col - local + (local + m) % span)

    def row_peer(span, k):
        local = row % span
        return (row - local + (local + k) % span, col)

    greeted = [col_peer(n_col, m) for m in range(1, n_col)]
    greeted += [row_peer(plan.n_row, k) for k in range(1, plan.n_row)]
    barrier = pltpu.get_barrier_semaphore()
    for peer in greeted:
        pl.semaphore_signal(barrier, inc=1, device_id=peer, device_id_type=MESH)

    loads = [
        pltpu.make_async_copy(source, target, in_sem.at[i])
        for i, (source, target) in enumerate(
            ((cor_hbm, cor), (er_hbm, er), (sh_hbm, sh), (x_hbm, xt))
        )
    ]
    for load in loads:
        load.start()

    def assembled_rows(start, count):
        total = None
        for k in range(kinds):
            ids = cor[k : k + 1, :]
            at = lax.broadcasted_iota(jnp.int32, (count, elems), 0) + start
            onehot = jnp.where(at == ids, 1.0, 0.0).astype(BF16)
            term = jnp.dot(onehot, er[k], preferred_element_type=F32)
            total = term if total is None else total + term
        return total

    loads[0].wait()
    loads[1].wait()
    halo_out[...] = assembled_rows(rows_dev, 2 * shared).reshape(halo_out.shape)
    own[...] = assembled_rows(0, rows_dev)
    pl.semaphore_wait(barrier, len(greeted))

    def remote(source, target, send, recv, peer):
        copy = pltpu.make_async_remote_copy(
            src_ref=source,
            dst_ref=target,
            send_sem=send,
            recv_sem=recv,
            device_id=peer,
            device_id_type=MESH,
        )
        copy.start()
        return copy

    sent = []
    halo = [
        remote(halo_out.at[1], halo_in.at[0], halo_s.at[0], halo_r.at[0], right),
        remote(halo_out.at[0], halo_in.at[1], halo_s.at[1], halo_r.at[1], left),
    ]
    sent += halo

    loads[2].wait()
    targets = jnp.concatenate([sh[0:1, :], sh[1:2, :]], axis=1)
    at = lax.broadcasted_iota(jnp.int32, (rows_dev, 2 * shared), 0)
    share_map = jnp.where(at == targets, 1.0, 0.0).astype(BF16)
    share_map = jnp.concatenate([share_map, share_map], axis=1)
    loads[3].wait()
    for copy in halo:
        copy.wait_recv()
    received = halo_in[...].reshape(2 * shared, -1)
    high = received.astype(BF16)
    low = (received - high.astype(F32)).astype(BF16)
    received = jnp.concatenate([high, low], axis=0)
    assembled = own[...] + jnp.dot(share_map, received, preferred_element_type=F32)
    rhs[...] = assembled.astype(BF16)
    part[...] = jnp.dot(xt[inner:, :], rhs[...], preferred_element_type=F32).reshape(part.shape)

    def own_rows(level, ahead=0):
        span, rows = plan.span(level), plan.piece(level)
        return pl.ds(pl.multiple_of((col % span + ahead) % span * rows, 8), rows)

    rs, ex, ag = {}, {}, {}
    for low, high in plan.groups:
        count = high - low + 1
        for m in range(1, plan.span(low)):
            rs[low, m] = remote(
                part.at[pl.ds(low - 1, count), own_rows(low, m)],
                rs_in.at[m - 1, pl.ds(low - 1, count), pl.ds(0, plan.piece(low))],
                rs_s.at[low - 1, m - 1],
                rs_r.at[low - 1, m - 1],
                col_peer(plan.span(low), m),
            )
    first = remote(part.at[0], l1_in, l1_s.at[0], l1_r.at[0], col_peer(2, 1))
    sent += list(rs.values()) + [first]

    weights = jnp.dot(xt[:inner, :], rhs[...], preferred_element_type=F32).astype(BF16)
    out_ref[...] = tdot(xt[:inner, :], weights)

    def gather(low, high):
        count = high - low + 1
        block = final.at[pl.ds(low - 1, count), own_rows(low)]
        for m in range(1, plan.span(low)):
            ag[low, m] = remote(
                block,
                block,
                ag_s.at[low - 1, m - 1],
                ag_r.at[low - 1, m - 1],
                col_peer(plan.span(low), m),
            )

    for low, high in plan.groups:
        rows = plan.piece(low)
        for m in range(1, plan.span(low)):
            rs[low, m].wait_recv()
        for level in range(low, high + 1):
            total = part[level - 1, own_rows(level)]
            for m in range(1, plan.span(low)):
                total = total + rs_in[m - 1, level - 1, pl.ds(0, rows)]
            if level <= plan.col_bits:
                final[level - 1, own_rows(level)] = total
            else:
                ex_out[level - plan.col_bits - 1] = total
        if low <= plan.col_bits:
            gather(low, high)
            continue
        for k in range(1, plan.n_row):
            for level in range(low, high + 1):
                if k < plan.row_span(level):
                    at_level = level - plan.col_bits - 1
                    ex[level, k] = remote(
                        ex_out.at[at_level],
                        ex_in.at[at_level, k - 1],
                        ex_s.at[at_level, k - 1],
                        ex_r.at[at_level, k - 1],
                        row_peer(plan.row_span(level), k),
                    )
    sent += list(ex.values())
    if plan.levels > plan.col_bits:
        low, high = plan.groups[0]
        for level in range(low, high + 1):
            at_level = level - plan.col_bits - 1
            total = ex_out[at_level]
            for k in range(1, plan.row_span(level)):
                ex[level, k].wait_recv()
                total = total + ex_in[at_level, k - 1]
            final[level - 1, own_rows(level)] = total
        gather(low, high)
    sent += list(ag.values())
    first.wait_recv()
    final[0] = part[0] + l1_in[...]
    for copy in ag.values():
        copy.wait_recv()
    coef = final[...].reshape(plan.sep * levels, -1).astype(BF16)
    out_ref[...] += tdot(xt[inner:, :], coef)
    for copy in sent:
        copy.wait_send()


def in_one_kernel(plan, elem_residual, corners, share_rows, x_factor):
    rows_dev, cols = x_factor.shape
    shared = share_rows.shape[2]
    elems, kinds, width = elem_residual.shape
    levels, sep = plan.levels, plan.sep
    slots = plan.n_col - 1
    row_levels = levels - plan.col_bits
    row_slots = plan.n_row - 1
    half = sep // 4
    small = sep // plan.n_col
    dma = pltpu.SemaphoreType.DMA
    anywhere = pl.BlockSpec(memory_space=pl.ANY)
    return pl.pallas_call(
        functools.partial(kernel, plan),
        out_shape=jax.ShapeDtypeStruct((rows_dev, width), F32),
        in_specs=[anywhere] * 4,
        out_specs=pl.BlockSpec(memory_space=pltpu.VMEM),
        scratch_shapes=[
            pltpu.VMEM((kinds, elems, width), BF16),
            pltpu.VMEM((kinds, elems), jnp.int32),
            pltpu.VMEM((2, shared), jnp.int32),
            pltpu.VMEM((cols, rows_dev), BF16),
            pltpu.VMEM((2, shared, width), F32),
            pltpu.VMEM((2, shared, width), F32),
            pltpu.VMEM((rows_dev, width), F32),
            pltpu.VMEM((rows_dev, width), BF16),
            pltpu.VMEM((levels, sep, width), F32),
            pltpu.VMEM((sep, width), F32),
            pltpu.VMEM((slots, levels, half, width), F32),
            pltpu.VMEM((row_levels, small, width), F32),
            pltpu.VMEM((row_levels, row_slots, small, width), F32),
            pltpu.VMEM((levels, sep, width), F32),
            dma((4,)),
            dma((2,)),
            dma((2,)),
            dma((1,)),
            dma((1,)),
            dma((levels, slots)),
            dma((levels, slots)),
            dma((row_levels, row_slots)),
            dma((row_levels, row_slots)),
            dma((levels, slots)),
            dma((levels, slots)),
        ],
        compiler_params=pltpu.CompilerParams(collective_id=0, has_side_effects=True),
        name="factor_solve",
    )(
        elem_residual.transpose(1, 0, 2),
        corners.T,
        share_rows.reshape(2, shared),
        x_factor.T,
    )


def solution(mesh):
    n_row, n_col = mesh.shape["row"], mesh.shape["col"]
    levels = (n_row * n_col).bit_length() - 1

    def per_device(elem_residual, corners, share_rows, x_factor):
        sep = (x_factor.shape[1] - INNER) // levels
        args = (elem_residual, corners, share_rows, x_factor)
        if takes(n_row, n_col, sep):
            return in_one_kernel(Plan(n_row, n_col, sep), *args)
        return by_rounds(n_row, n_col, *args)

    placed = (
        P(("row", "col"), None, None),
        P(("row", "col"), None),
        P(("row", "col"), None, None),
        P(("row", "col"), None),
    )
    return jax.shard_map(
        per_device, mesh=mesh, in_specs=placed, out_specs=P(("row", "col"), None), check_vma=False
    )
```

```python
import functools

import jax
import jax.numpy as jnp
from jax import lax
from jax.experimental import pallas as pl
from jax.experimental.pallas import tpu as pltpu
from jax.sharding import PartitionSpec as P

INNER = 1408
MESH = pl.DeviceIdType.MESH
F32 = jnp.float32
BF16 = jnp.bfloat16


def swapped(block, axis, stride):
    count = lax.axis_size(axis)
    route = []
    for low in range(count):
        high = low | 1 << stride
        if high != low and high < count:
            route += [(low, high), (high, low)]
    return lax.ppermute(block, axis, route)


def summed_levels(blocks, n_row, n_col):
    col_bits = n_col.bit_length() - 1
    row_bits = n_row.bit_length() - 1
    for bit in range(col_bits + row_bits):
        axis, stride = ("col", bit) if bit < col_bits else ("row", bit - col_bits)
        partner = swapped(blocks[bit:], axis, stride)
        blocks = jnp.concatenate([blocks[:bit], blocks[bit:] + partner], axis=0)
    return blocks


def by_rounds(n_row, n_col, elem_residual, corners, share_rows, x_factor):
    rows_dev = x_factor.shape[0]
    shared = share_rows.shape[2]
    width = elem_residual.shape[2]
    levels = (n_row * n_col).bit_length() - 1
    ext_len = rows_dev + 2 * shared
    flat_ids = corners.reshape(-1)
    onehot = (
        lax.broadcasted_iota(jnp.int32, (ext_len, flat_ids.shape[0]), 0) == flat_ids[None, :]
    ).astype(BF16)
    extended = jnp.dot(onehot, elem_residual.reshape(-1, width), preferred_element_type=F32)
    forward = [(i, (i + 1) % n_col) for i in range(n_col)]
    backward = [(target, source) for source, target in forward]
    from_left = lax.ppermute(extended[rows_dev + shared :], "col", forward)
    from_right = lax.ppermute(extended[rows_dev : rows_dev + shared], "col", backward)
    row_ids = lax.broadcasted_iota(jnp.int32, (rows_dev, shared), 0)
    assembled = extended[:rows_dev]
    for side, received in ((0, from_left), (1, from_right)):
        side_map = (row_ids == share_rows[0, side][None, :]).astype(F32)
        assembled = assembled + jnp.dot(
            side_map, received, precision=lax.Precision.HIGHEST, preferred_element_type=F32
        )
    partial_value = lax.dot_general(
        x_factor, assembled.astype(BF16), (((0,), (0,)), ((), ())), preferred_element_type=F32
    )
    blocks = partial_value[INNER:].reshape(levels, -1, width)
    blocks = summed_levels(blocks, n_row, n_col)
    coef = jnp.concatenate([partial_value[:INNER], blocks.reshape(-1, width)], axis=0)
    return jnp.dot(x_factor, coef.astype(BF16), preferred_element_type=F32)


class Plan:
    def __init__(self, n_row, n_col, sep):
        self.n_row, self.n_col, self.sep = n_row, n_col, sep
        self.levels = (n_row * n_col).bit_length() - 1
        self.col_bits = n_col.bit_length() - 1
        self.groups = []
        if self.levels > self.col_bits:
            self.groups.append((self.col_bits + 1, self.levels))
        self.groups += [(level, level) for level in range(self.col_bits, 1, -1)]

    def span(self, level):
        return min(2**level, self.n_col)

    def row_span(self, level):
        return max(1, 2**level // self.n_col)

    def piece(self, level):
        return self.sep // self.span(level)


def takes(n_row, n_col, sep):
    return n_col >= 4 and 2 <= n_row <= 4 and sep % (8 * n_col) == 0


def tdot(a, b):
    return lax.dot_general(a, b, (((0,), (0,)), ((), ())), preferred_element_type=F32)


def kernel(
    plan,
    er_hbm, cor_hbm, sh_hbm, x_hbm,
    out_ref,
    er, cor, sh, xt,
    halo_out, halo_in, own, rhs, part, l1_in, rs_in, ex_out, ex_in, final,
    in_sem, halo_s, halo_r, l1_s, l1_r, rs_s, rs_r, ex_s, ex_r, ag_s, ag_r,
):
    row, col = lax.axis_index("row"), lax.axis_index("col")
    levels, n_col = plan.levels, plan.n_col
    rows_dev = out_ref.shape[0]
    shared = halo_out.shape[1]
    kinds = er.shape[0]
    elems = er.shape[1]
    inner = xt.shape[0] - plan.sep * levels

    right = (row, (col + 1) % n_col)
    left = (row, (col + n_col - 1) % n_col)

    def col_peer(span, m):
        local = col % span
        return (row, col - local + (local + m) % span)

    def row_peer(span, k):
        local = row % span
        return (row - local + (local + k) % span, col)

    greeted = [col_peer(n_col, m) for m in range(1, n_col)]
    greeted += [row_peer(plan.n_row, k) for k in range(1, plan.n_row)]
    barrier = pltpu.get_barrier_semaphore()
    for peer in greeted:
        pl.semaphore_signal(barrier, inc=1, device_id=peer, device_id_type=MESH)

    loads = [
        pltpu.make_async_copy(source, target, in_sem.at[i])
        for i, (source, target) in enumerate(
            ((cor_hbm, cor), (er_hbm, er), (sh_hbm, sh), (x_hbm, xt))
        )
    ]
    for load in loads:
        load.start()

    def assembled_rows(start, count):
        total = None
        for k in range(kinds):
            ids = cor[k : k + 1, :]
            at = lax.broadcasted_iota(jnp.int32, (count, elems), 0) + start
            onehot = jnp.where(at == ids, 1.0, 0.0).astype(BF16)
            term = jnp.dot(onehot, er[k], preferred_element_type=F32)
            total = term if total is None else total + term
        return total

    loads[0].wait()
    loads[1].wait()
    halo_out[...] = assembled_rows(rows_dev, 2 * shared).reshape(halo_out.shape)
    own[...] = assembled_rows(0, rows_dev)
    pl.semaphore_wait(barrier, len(greeted))

    def remote(source, target, send, recv, peer):
        copy = pltpu.make_async_remote_copy(
            src_ref=source,
            dst_ref=target,
            send_sem=send,
            recv_sem=recv,
            device_id=peer,
            device_id_type=MESH,
        )
        copy.start()
        return copy

    sent = []
    halo = [
        remote(halo_out.at[1], halo_in.at[0], halo_s.at[0], halo_r.at[0], right),
        remote(halo_out.at[0], halo_in.at[1], halo_s.at[1], halo_r.at[1], left),
    ]
    sent += halo

    loads[2].wait()
    targets = jnp.concatenate([sh[0:1, :], sh[1:2, :]], axis=1)
    at = lax.broadcasted_iota(jnp.int32, (rows_dev, 2 * shared), 0)
    share_map = jnp.where(at == targets, 1.0, 0.0).astype(BF16)
    share_map = jnp.concatenate([share_map, share_map], axis=1)
    loads[3].wait()
    for copy in halo:
        copy.wait_recv()
    received = halo_in[...].reshape(2 * shared, -1)
    high = received.astype(BF16)
    low = (received - high.astype(F32)).astype(BF16)
    received = jnp.concatenate([high, low], axis=0)
    assembled = own[...] + jnp.dot(share_map, received, preferred_element_type=F32)
    rhs[...] = assembled.astype(BF16)
    part[...] = jnp.dot(xt[inner:, :], rhs[...], preferred_element_type=F32).reshape(part.shape)

    def own_rows(level, ahead=0):
        span, rows = plan.span(level), plan.piece(level)
        return pl.ds(pl.multiple_of((col % span + ahead) % span * rows, 8), rows)

    rs, ex, ag = {}, {}, {}
    for low, high in plan.groups:
        count = high - low + 1
        for m in range(1, plan.span(low)):
            rs[low, m] = remote(
                part.at[pl.ds(low - 1, count), own_rows(low, m)],
                rs_in.at[m - 1, pl.ds(low - 1, count), pl.ds(0, plan.piece(low))],
                rs_s.at[low - 1, m - 1],
                rs_r.at[low - 1, m - 1],
                col_peer(plan.span(low), m),
            )
    first = remote(part.at[0], l1_in, l1_s.at[0], l1_r.at[0], col_peer(2, 1))
    sent += list(rs.values()) + [first]

    weights = jnp.dot(xt[:inner, :], rhs[...], preferred_element_type=F32).astype(BF16)
    out_ref[...] = tdot(xt[:inner, :], weights)

    def gather(low, high):
        count = high - low + 1
        block = final.at[pl.ds(low - 1, count), own_rows(low)]
        for m in range(1, plan.span(low)):
            ag[low, m] = remote(
                block,
                block,
                ag_s.at[low - 1, m - 1],
                ag_r.at[low - 1, m - 1],
                col_peer(plan.span(low), m),
            )

    for low, high in plan.groups:
        rows = plan.piece(low)
        for m in range(1, plan.span(low)):
            rs[low, m].wait_recv()
        for level in range(low, high + 1):
            total = part[level - 1, own_rows(level)]
            for m in range(1, plan.span(low)):
                total = total + rs_in[m - 1, level - 1, pl.ds(0, rows)]
            if level <= plan.col_bits:
                final[level - 1, own_rows(level)] = total
            else:
                ex_out[level - plan.col_bits - 1] = total
        if low <= plan.col_bits:
            gather(low, high)
            continue
        for k in range(1, plan.n_row):
            for level in range(low, high + 1):
                if k < plan.row_span(level):
                    at_level = level - plan.col_bits - 1
                    ex[level, k] = remote(
                        ex_out.at[at_level],
                        ex_in.at[at_level, k - 1],
                        ex_s.at[at_level, k - 1],
                        ex_r.at[at_level, k - 1],
                        row_peer(plan.row_span(level), k),
                    )
    sent += list(ex.values())
    if plan.levels > plan.col_bits:
        low, high = plan.groups[0]
        for level in range(low, high + 1):
            at_level = level - plan.col_bits - 1
            total = ex_out[at_level]
            for k in range(1, plan.row_span(level)):
                ex[level, k].wait_recv()
                total = total + ex_in[at_level, k - 1]
            final[level - 1, own_rows(level)] = total
        gather(low, high)
    sent += list(ag.values())
    first.wait_recv()
    final[0] = part[0] + l1_in[...]
    for copy in ag.values():
        copy.wait_recv()
    coef = final[...].reshape(plan.sep * levels, -1).astype(BF16)
    out_ref[...] += tdot(xt[inner:, :], coef)
    for copy in sent:
        copy.wait_send()


def in_one_kernel(plan, elem_residual, corners, share_rows, x_factor):
    rows_dev, cols = x_factor.shape
    shared = share_rows.shape[2]
    elems, kinds, width = elem_residual.shape
    levels, sep = plan.levels, plan.sep
    slots = plan.n_col - 1
    row_levels = levels - plan.col_bits
    row_slots = plan.n_row - 1
    half = sep // 4
    small = sep // plan.n_col
    dma = pltpu.SemaphoreType.DMA
    anywhere = pl.BlockSpec(memory_space=pl.ANY)
    return pl.pallas_call(
        functools.partial(kernel, plan),
        out_shape=pltpu.VMEM((rows_dev, width), F32),
        in_specs=[anywhere] * 4,
        out_specs=pl.BlockSpec(memory_space=pltpu.VMEM),
        scratch_shapes=[
            pltpu.VMEM((kinds, elems, width), BF16),
            pltpu.VMEM((kinds, elems), jnp.int32),
            pltpu.VMEM((2, shared), jnp.int32),
            pltpu.VMEM((cols, rows_dev), BF16),
            pltpu.VMEM((2, shared, width), F32),
            pltpu.VMEM((2, shared, width), F32),
            pltpu.VMEM((rows_dev, width), F32),
            pltpu.VMEM((rows_dev, width), BF16),
            pltpu.VMEM((levels, sep, width), F32),
            pltpu.VMEM((sep, width), F32),
            pltpu.VMEM((slots, levels, half, width), F32),
            pltpu.VMEM((row_levels, small, width), F32),
            pltpu.VMEM((row_levels, row_slots, small, width), F32),
            pltpu.VMEM((levels, sep, width), F32),
            dma((4,)),
            dma((2,)),
            dma((2,)),
            dma((1,)),
            dma((1,)),
            dma((levels, slots)),
            dma((levels, slots)),
            dma((row_levels, row_slots)),
            dma((row_levels, row_slots)),
            dma((levels, slots)),
            dma((levels, slots)),
        ],
        compiler_params=pltpu.CompilerParams(collective_id=0, has_side_effects=True),
        name="factor_solve",
    )(
        elem_residual.transpose(1, 0, 2),
        corners.T,
        share_rows.reshape(2, shared),
        x_factor.T,
    )


def solution(mesh):
    n_row, n_col = mesh.shape["row"], mesh.shape["col"]
    levels = (n_row * n_col).bit_length() - 1

    def per_device(elem_residual, corners, share_rows, x_factor):
        sep = (x_factor.shape[1] - INNER) // levels
        args = (elem_residual, corners, share_rows, x_factor)
        if takes(n_row, n_col, sep):
            return in_one_kernel(Plan(n_row, n_col, sep), *args)
        return by_rounds(n_row, n_col, *args)

    placed = (
        P(("row", "col"), None, None),
        P(("row", "col"), None),
        P(("row", "col"), None, None),
        P(("row", "col"), None),
    )
    return jax.shard_map(
        per_device, mesh=mesh, in_specs=placed, out_specs=P(("row", "col"), None), check_vma=False
    )
```

```python
import functools

import jax
import jax.numpy as jnp
from jax import lax
from jax.experimental import pallas as pl
from jax.experimental.pallas import tpu as pltpu
from jax.sharding import PartitionSpec as P

INNER = 1408
MESH = pl.DeviceIdType.MESH
F32 = jnp.float32
BF16 = jnp.bfloat16


def swapped(block, axis, stride):
    count = lax.axis_size(axis)
    route = []
    for low in range(count):
        high = low | 1 << stride
        if high != low and high < count:
            route += [(low, high), (high, low)]
    return lax.ppermute(block, axis, route)


def summed_levels(blocks, n_row, n_col):
    col_bits = n_col.bit_length() - 1
    row_bits = n_row.bit_length() - 1
    for bit in range(col_bits + row_bits):
        axis, stride = ("col", bit) if bit < col_bits else ("row", bit - col_bits)
        partner = swapped(blocks[bit:], axis, stride)
        blocks = jnp.concatenate([blocks[:bit], blocks[bit:] + partner], axis=0)
    return blocks


def by_rounds(n_row, n_col, elem_residual, corners, share_rows, x_factor):
    rows_dev = x_factor.shape[0]
    shared = share_rows.shape[2]
    width = elem_residual.shape[2]
    levels = (n_row * n_col).bit_length() - 1
    ext_len = rows_dev + 2 * shared
    flat_ids = corners.reshape(-1)
    onehot = (
        lax.broadcasted_iota(jnp.int32, (ext_len, flat_ids.shape[0]), 0) == flat_ids[None, :]
    ).astype(BF16)
    extended = jnp.dot(onehot, elem_residual.reshape(-1, width), preferred_element_type=F32)
    forward = [(i, (i + 1) % n_col) for i in range(n_col)]
    backward = [(target, source) for source, target in forward]
    from_left = lax.ppermute(extended[rows_dev + shared :], "col", forward)
    from_right = lax.ppermute(extended[rows_dev : rows_dev + shared], "col", backward)
    row_ids = lax.broadcasted_iota(jnp.int32, (rows_dev, shared), 0)
    assembled = extended[:rows_dev]
    for side, received in ((0, from_left), (1, from_right)):
        side_map = (row_ids == share_rows[0, side][None, :]).astype(F32)
        assembled = assembled + jnp.dot(
            side_map, received, precision=lax.Precision.HIGHEST, preferred_element_type=F32
        )
    partial_value = lax.dot_general(
        x_factor, assembled.astype(BF16), (((0,), (0,)), ((), ())), preferred_element_type=F32
    )
    blocks = partial_value[INNER:].reshape(levels, -1, width)
    blocks = summed_levels(blocks, n_row, n_col)
    coef = jnp.concatenate([partial_value[:INNER], blocks.reshape(-1, width)], axis=0)
    return jnp.dot(x_factor, coef.astype(BF16), preferred_element_type=F32)


class Plan:
    def __init__(self, n_row, n_col, sep):
        self.n_row, self.n_col, self.sep = n_row, n_col, sep
        self.levels = (n_row * n_col).bit_length() - 1
        self.col_bits = n_col.bit_length() - 1
        self.groups = []
        if self.levels > self.col_bits:
            self.groups.append((self.col_bits + 1, self.levels))
        self.groups += [(level, level) for level in range(self.col_bits, 1, -1)]

    def span(self, level):
        return min(2**level, self.n_col)

    def row_span(self, level):
        return max(1, 2**level // self.n_col)

    def piece(self, level):
        return self.sep // self.span(level)


def takes(n_row, n_col, sep):
    return n_col >= 4 and 2 <= n_row <= 4 and sep % (8 * n_col) == 0


def tdot(a, b):
    return lax.dot_general(a, b, (((0,), (0,)), ((), ())), preferred_element_type=F32)


def kernel(
    plan,
    er_hbm, cor_hbm, sh_hbm, x_hbm,
    out_ref,
    er, cor, sh, xt,
    halo_out, halo_in, own, rhs, part, l1_in, rs_in, ex_out, ex_in, final, turned,
    in_sem, halo_s, halo_r, l1_s, l1_r, rs_s, rs_r, ex_s, ex_r, ag_s, ag_r,
):
    row, col = lax.axis_index("row"), lax.axis_index("col")
    levels, n_col = plan.levels, plan.n_col
    rows_dev = out_ref.shape[0]
    shared = halo_out.shape[1]
    kinds = er.shape[0]
    elems = er.shape[1]
    inner = xt.shape[0] - plan.sep * levels

    right = (row, (col + 1) % n_col)
    left = (row, (col + n_col - 1) % n_col)

    def col_peer(span, m):
        local = col % span
        return (row, col - local + (local + m) % span)

    def row_peer(span, k):
        local = row % span
        return (row - local + (local + k) % span, col)

    greeted = [col_peer(n_col, m) for m in range(1, n_col)]
    greeted += [row_peer(plan.n_row, k) for k in range(1, plan.n_row)]
    barrier = pltpu.get_barrier_semaphore()
    for peer in greeted:
        pl.semaphore_signal(barrier, inc=1, device_id=peer, device_id_type=MESH)

    loads = [
        pltpu.make_async_copy(source, target, in_sem.at[i])
        for i, (source, target) in enumerate(
            ((cor_hbm, cor), (er_hbm, er), (sh_hbm, sh), (x_hbm, xt))
        )
    ]
    for load in loads:
        load.start()

    def assembled_rows(start, count):
        total = None
        for k in range(kinds):
            ids = cor[k : k + 1, :]
            at = lax.broadcasted_iota(jnp.int32, (count, elems), 0) + start
            onehot = jnp.where(at == ids, 1.0, 0.0).astype(BF16)
            term = jnp.dot(onehot, er[k], preferred_element_type=F32)
            total = term if total is None else total + term
        return total

    loads[0].wait()
    loads[1].wait()
    halo_out[...] = assembled_rows(rows_dev, 2 * shared).reshape(halo_out.shape)
    own[...] = assembled_rows(0, rows_dev)
    pl.semaphore_wait(barrier, len(greeted))

    def remote(source, target, send, recv, peer):
        copy = pltpu.make_async_remote_copy(
            src_ref=source,
            dst_ref=target,
            send_sem=send,
            recv_sem=recv,
            device_id=peer,
            device_id_type=MESH,
        )
        copy.start()
        return copy

    sent = []
    halo = [
        remote(halo_out.at[1], halo_in.at[0], halo_s.at[0], halo_r.at[0], right),
        remote(halo_out.at[0], halo_in.at[1], halo_s.at[1], halo_r.at[1], left),
    ]
    sent += halo

    loads[2].wait()
    targets = jnp.concatenate([sh[0:1, :], sh[1:2, :]], axis=1)
    at = lax.broadcasted_iota(jnp.int32, (rows_dev, 2 * shared), 0)
    share_map = jnp.where(at == targets, 1.0, 0.0).astype(BF16)
    share_map = jnp.concatenate([share_map, share_map], axis=1)
    loads[3].wait()
    for copy in halo:
        copy.wait_recv()
    received = halo_in[...].reshape(2 * shared, -1)
    high = received.astype(BF16)
    low = (received - high.astype(F32)).astype(BF16)
    received = jnp.concatenate([high, low], axis=0)
    assembled = own[...] + jnp.dot(share_map, received, preferred_element_type=F32)
    rhs[...] = assembled.astype(BF16)

    def partial(low, high):
        rows = xt[inner + plan.sep * (low - 1) : inner + plan.sep * high, :]
        block = jnp.dot(rows, rhs[...], preferred_element_type=F32)
        part[low - 1 : high] = block.reshape(high - low + 1, plan.sep, -1)


    def own_rows(level, ahead=0):
        span, rows = plan.span(level), plan.piece(level)
        return pl.ds(pl.multiple_of((col % span + ahead) % span * rows, 8), rows)

    rs, ex, ag = {}, {}, {}
    def scatter(low, high):
        count = high - low + 1
        for m in range(1, plan.span(low)):
            rs[low, m] = remote(
                part.at[pl.ds(low - 1, count), own_rows(low, m)],
                rs_in.at[m - 1, pl.ds(low - 1, count), pl.ds(0, plan.piece(low))],
                rs_s.at[low - 1, m - 1],
                rs_r.at[low - 1, m - 1],
                col_peer(plan.span(low), m),
            )
    partial(*plan.groups[0])
    scatter(*plan.groups[0])
    partial(1, plan.col_bits)
    weights = jnp.dot(xt[:inner, :], rhs[...], preferred_element_type=F32).astype(BF16)
    out_ref[...] = tdot(xt[:inner, :], weights)
    for group in plan.groups[1:]:
        scatter(*group)
    turned[...] = xt[inner:, :].T
    sent += list(rs.values())

    def gather(low, high):
        count = high - low + 1
        block = final.at[pl.ds(low - 1, count), own_rows(low)]
        for m in range(1, plan.span(low)):
            ag[low, m] = remote(
                block,
                block,
                ag_s.at[low - 1, m - 1],
                ag_r.at[low - 1, m - 1],
                col_peer(plan.span(low), m),
            )

    for low, high in plan.groups:
        rows = plan.piece(low)
        for m in range(1, plan.span(low)):
            rs[low, m].wait_recv()
        for level in range(low, high + 1):
            total = part[level - 1, own_rows(level)]
            for m in range(1, plan.span(low)):
                total = total + rs_in[m - 1, level - 1, pl.ds(0, rows)]
            if level <= plan.col_bits:
                final[level - 1, own_rows(level)] = total
            else:
                ex_out[level - plan.col_bits - 1] = total
        if low <= plan.col_bits:
            gather(low, high)
            continue
        for k in range(1, plan.n_row):
            for level in range(low, high + 1):
                if k < plan.row_span(level):
                    at_level = level - plan.col_bits - 1
                    ex[level, k] = remote(
                        ex_out.at[at_level],
                        ex_in.at[at_level, k - 1],
                        ex_s.at[at_level, k - 1],
                        ex_r.at[at_level, k - 1],
                        row_peer(plan.row_span(level), k),
                    )
    first = remote(part.at[0], l1_in, l1_s.at[0], l1_r.at[0], col_peer(2, 1))
    sent += list(ex.values()) + [first]
    if plan.levels > plan.col_bits:
        low, high = plan.groups[0]
        for level in range(low, high + 1):
            at_level = level - plan.col_bits - 1
            total = ex_out[at_level]
            for k in range(1, plan.row_span(level)):
                ex[level, k].wait_recv()
                total = total + ex_in[at_level, k - 1]
            final[level - 1, own_rows(level)] = total
            gather(level, level)
    sent += list(ag.values())

    def applied(low, high):
        coef = final[low - 1 : high].reshape(plan.sep * (high - low + 1), -1).astype(BF16)
        return jnp.dot(turned[:, plan.sep * (low - 1) : plan.sep * high], coef, preferred_element_type=F32)

    first.wait_recv()
    final[0] = part[0] + l1_in[...]
    for (low, m), copy in ag.items():
        if low < plan.groups[0][0]:
            copy.wait_recv()
    out_ref[...] += applied(1, plan.col_bits)
    for (low, m), copy in ag.items():
        if low >= plan.groups[0][0]:
            copy.wait_recv()
    out_ref[...] += applied(*plan.groups[0])
    for copy in sent:
        copy.wait_send()


def in_one_kernel(plan, elem_residual, corners, share_rows, x_factor):
    rows_dev, cols = x_factor.shape
    shared = share_rows.shape[2]
    elems, kinds, width = elem_residual.shape
    levels, sep = plan.levels, plan.sep
    slots = plan.n_col - 1
    row_levels = levels - plan.col_bits
    row_slots = plan.n_row - 1
    half = sep // 4
    small = sep // plan.n_col
    dma = pltpu.SemaphoreType.DMA
    anywhere = pl.BlockSpec(memory_space=pl.ANY)
    return pl.pallas_call(
        functools.partial(kernel, plan),
        out_shape=pltpu.VMEM((rows_dev, width), F32),
        in_specs=[anywhere] * 4,
        out_specs=pl.BlockSpec(memory_space=pltpu.VMEM),
        scratch_shapes=[
            pltpu.VMEM((kinds, elems, width), BF16),
            pltpu.VMEM((kinds, elems), jnp.int32),
            pltpu.VMEM((2, shared), jnp.int32),
            pltpu.VMEM((cols, rows_dev), BF16),
            pltpu.VMEM((2, shared, width), F32),
            pltpu.VMEM((2, shared, width), F32),
            pltpu.VMEM((rows_dev, width), F32),
            pltpu.VMEM((rows_dev, width), BF16),
            pltpu.VMEM((levels, sep, width), F32),
            pltpu.VMEM((sep, width), F32),
            pltpu.VMEM((slots, levels, half, width), F32),
            pltpu.VMEM((row_levels, small, width), F32),
            pltpu.VMEM((row_levels, row_slots, small, width), F32),
            pltpu.VMEM((levels, sep, width), F32),
            pltpu.VMEM((rows_dev, sep * levels), BF16),
            dma((4,)),
            dma((2,)),
            dma((2,)),
            dma((1,)),
            dma((1,)),
            dma((levels, slots)),
            dma((levels, slots)),
            dma((row_levels, row_slots)),
            dma((row_levels, row_slots)),
            dma((levels, slots)),
            dma((levels, slots)),
        ],
        compiler_params=pltpu.CompilerParams(collective_id=0, has_side_effects=True),
        name="factor_solve",
    )(
        elem_residual.transpose(1, 0, 2),
        corners.T,
        share_rows.reshape(2, shared),
        x_factor.T,
    )


def solution(mesh):
    n_row, n_col = mesh.shape["row"], mesh.shape["col"]
    levels = (n_row * n_col).bit_length() - 1

    def per_device(elem_residual, corners, share_rows, x_factor):
        sep = (x_factor.shape[1] - INNER) // levels
        args = (elem_residual, corners, share_rows, x_factor)
        if takes(n_row, n_col, sep):
            return in_one_kernel(Plan(n_row, n_col, sep), *args)
        return by_rounds(n_row, n_col, *args)

    placed = (
        P(("row", "col"), None, None),
        P(("row", "col"), None),
        P(("row", "col"), None, None),
        P(("row", "col"), None),
    )
    return jax.shard_map(
        per_device, mesh=mesh, in_specs=placed, out_specs=P(("row", "col"), None), check_vma=False
    )
```

```python
import functools

import jax
import jax.numpy as jnp
from jax import lax
from jax.experimental import pallas as pl
from jax.experimental.pallas import tpu as pltpu
from jax.sharding import PartitionSpec as P

INNER = 1408
MESH = pl.DeviceIdType.MESH
F32 = jnp.float32
BF16 = jnp.bfloat16


def swapped(block, axis, stride):
    count = lax.axis_size(axis)
    route = []
    for low in range(count):
        high = low | 1 << stride
        if high != low and high < count:
            route += [(low, high), (high, low)]
    return lax.ppermute(block, axis, route)


def summed_levels(blocks, n_row, n_col):
    col_bits = n_col.bit_length() - 1
    row_bits = n_row.bit_length() - 1
    for bit in range(col_bits + row_bits):
        axis, stride = ("col", bit) if bit < col_bits else ("row", bit - col_bits)
        partner = swapped(blocks[bit:], axis, stride)
        blocks = jnp.concatenate([blocks[:bit], blocks[bit:] + partner], axis=0)
    return blocks


def by_rounds(n_row, n_col, elem_residual, corners, share_rows, x_factor):
    rows_dev = x_factor.shape[0]
    shared = share_rows.shape[2]
    width = elem_residual.shape[2]
    levels = (n_row * n_col).bit_length() - 1
    ext_len = rows_dev + 2 * shared
    flat_ids = corners.reshape(-1)
    onehot = (
        lax.broadcasted_iota(jnp.int32, (ext_len, flat_ids.shape[0]), 0) == flat_ids[None, :]
    ).astype(BF16)
    extended = jnp.dot(onehot, elem_residual.reshape(-1, width), preferred_element_type=F32)
    forward = [(i, (i + 1) % n_col) for i in range(n_col)]
    backward = [(target, source) for source, target in forward]
    from_left = lax.ppermute(extended[rows_dev + shared :], "col", forward)
    from_right = lax.ppermute(extended[rows_dev : rows_dev + shared], "col", backward)
    row_ids = lax.broadcasted_iota(jnp.int32, (rows_dev, shared), 0)
    assembled = extended[:rows_dev]
    for side, received in ((0, from_left), (1, from_right)):
        side_map = (row_ids == share_rows[0, side][None, :]).astype(F32)
        assembled = assembled + jnp.dot(
            side_map, received, precision=lax.Precision.HIGHEST, preferred_element_type=F32
        )
    partial_value = lax.dot_general(
        x_factor, assembled.astype(BF16), (((0,), (0,)), ((), ())), preferred_element_type=F32
    )
    blocks = partial_value[INNER:].reshape(levels, -1, width)
    blocks = summed_levels(blocks, n_row, n_col)
    coef = jnp.concatenate([partial_value[:INNER], blocks.reshape(-1, width)], axis=0)
    return jnp.dot(x_factor, coef.astype(BF16), preferred_element_type=F32)


class Plan:
    def __init__(self, n_row, n_col, sep):
        self.n_row, self.n_col, self.sep = n_row, n_col, sep
        self.levels = (n_row * n_col).bit_length() - 1
        self.col_bits = n_col.bit_length() - 1
        self.groups = []
        if self.levels > self.col_bits:
            self.groups += [(level, level) for level in range(self.levels, self.col_bits, -1)]
        self.groups += [(level, level) for level in range(self.col_bits, 1, -1)]

    def span(self, level):
        return min(2**level, self.n_col)

    def row_span(self, level):
        return max(1, 2**level // self.n_col)

    def piece(self, level):
        return self.sep // self.span(level)


def takes(n_row, n_col, sep):
    return n_col >= 4 and 2 <= n_row <= 4 and sep % (8 * n_col) == 0


def tdot(a, b):
    return lax.dot_general(a, b, (((0,), (0,)), ((), ())), preferred_element_type=F32)


def kernel(
    plan,
    er_hbm, cor_hbm, sh_hbm, x_hbm,
    out_ref,
    er, cor, sh, xt,
    halo_out, halo_in, own, rhs, part, l1_in, rs_in, ex_out, ex_in, final, turned,
    in_sem, halo_s, halo_r, l1_s, l1_r, rs_s, rs_r, ex_s, ex_r, ag_s, ag_r,
):
    row, col = lax.axis_index("row"), lax.axis_index("col")
    levels, n_col = plan.levels, plan.n_col
    rows_dev = out_ref.shape[0]
    shared = halo_out.shape[1]
    kinds = er.shape[0]
    elems = er.shape[1]
    inner = xt.shape[0] - plan.sep * levels

    right = (row, (col + 1) % n_col)
    left = (row, (col + n_col - 1) % n_col)

    def col_peer(span, m):
        local = col % span
        return (row, col - local + (local + m) % span)

    def row_peer(span, k):
        local = row % span
        return (row - local + (local + k) % span, col)

    greeted = [col_peer(n_col, m) for m in range(1, n_col)]
    greeted += [row_peer(plan.n_row, k) for k in range(1, plan.n_row)]
    barrier = pltpu.get_barrier_semaphore()
    for peer in greeted:
        pl.semaphore_signal(barrier, inc=1, device_id=peer, device_id_type=MESH)

    loads = [
        pltpu.make_async_copy(source, target, in_sem.at[i])
        for i, (source, target) in enumerate(
            ((cor_hbm, cor), (er_hbm, er), (sh_hbm, sh), (x_hbm, xt))
        )
    ]
    for load in loads:
        load.start()

    def assembled_rows(start, count):
        total = None
        for k in range(kinds):
            ids = cor[k : k + 1, :]
            at = lax.broadcasted_iota(jnp.int32, (count, elems), 0) + start
            onehot = jnp.where(at == ids, 1.0, 0.0).astype(BF16)
            term = jnp.dot(onehot, er[k], preferred_element_type=F32)
            total = term if total is None else total + term
        return total

    loads[0].wait()
    loads[1].wait()
    halo_out[...] = assembled_rows(rows_dev, 2 * shared).reshape(halo_out.shape)
    own[...] = assembled_rows(0, rows_dev)
    pl.semaphore_wait(barrier, len(greeted))

    def remote(source, target, send, recv, peer):
        copy = pltpu.make_async_remote_copy(
            src_ref=source,
            dst_ref=target,
            send_sem=send,
            recv_sem=recv,
            device_id=peer,
            device_id_type=MESH,
        )
        copy.start()
        return copy

    sent = []
    halo = [
        remote(halo_out.at[1], halo_in.at[0], halo_s.at[0], halo_r.at[0], right),
        remote(halo_out.at[0], halo_in.at[1], halo_s.at[1], halo_r.at[1], left),
    ]
    sent += halo

    loads[2].wait()
    targets = jnp.concatenate([sh[0:1, :], sh[1:2, :]], axis=1)
    at = lax.broadcasted_iota(jnp.int32, (rows_dev, 2 * shared), 0)
    share_map = jnp.where(at == targets, 1.0, 0.0).astype(BF16)
    share_map = jnp.concatenate([share_map, share_map], axis=1)
    loads[3].wait()
    for copy in halo:
        copy.wait_recv()
    received = halo_in[...].reshape(2 * shared, -1)
    high = received.astype(BF16)
    low = (received - high.astype(F32)).astype(BF16)
    received = jnp.concatenate([high, low], axis=0)
    assembled = own[...] + jnp.dot(share_map, received, preferred_element_type=F32)
    rhs[...] = assembled.astype(BF16)

    def partial(low, high):
        rows = xt[inner + plan.sep * (low - 1) : inner + plan.sep * high, :]
        block = jnp.dot(rows, rhs[...], preferred_element_type=F32)
        part[low - 1 : high] = block.reshape(high - low + 1, plan.sep, -1)


    def own_rows(level, ahead=0):
        span, rows = plan.span(level), plan.piece(level)
        return pl.ds(pl.multiple_of((col % span + ahead) % span * rows, 8), rows)

    rs, ex, ag = {}, {}, {}
    def scatter(low, high):
        count = high - low + 1
        for m in range(1, plan.span(low)):
            rs[low, m] = remote(
                part.at[pl.ds(low - 1, count), own_rows(low, m)],
                rs_in.at[m - 1, pl.ds(low - 1, count), pl.ds(0, plan.piece(low))],
                rs_s.at[low - 1, m - 1],
                rs_r.at[low - 1, m - 1],
                col_peer(plan.span(low), m),
            )
    partial(plan.col_bits + 1, levels)
    for group in plan.groups:
        if group[0] > plan.col_bits:
            scatter(*group)
    partial(1, plan.col_bits)
    weights = jnp.dot(xt[:inner, :], rhs[...], preferred_element_type=F32).astype(BF16)
    out_ref[...] = tdot(xt[:inner, :], weights)
    for group in plan.groups:
        if group[0] <= plan.col_bits:
            scatter(*group)
    turned[...] = xt[inner:, :].T
    sent += list(rs.values())

    def gather(low, high):
        count = high - low + 1
        block = final.at[pl.ds(low - 1, count), own_rows(low)]
        for m in range(1, plan.span(low)):
            ag[low, m] = remote(
                block,
                block,
                ag_s.at[low - 1, m - 1],
                ag_r.at[low - 1, m - 1],
                col_peer(plan.span(low), m),
            )

    for low, high in plan.groups:
        rows = plan.piece(low)
        for m in range(1, plan.span(low)):
            rs[low, m].wait_recv()
        for level in range(low, high + 1):
            total = part[level - 1, own_rows(level)]
            for m in range(1, plan.span(low)):
                total = total + rs_in[m - 1, level - 1, pl.ds(0, rows)]
            if level <= plan.col_bits:
                final[level - 1, own_rows(level)] = total
            else:
                ex_out[level - plan.col_bits - 1] = total
        if low <= plan.col_bits:
            gather(low, high)
            continue
        for k in range(1, plan.n_row):
            for level in range(low, high + 1):
                if k < plan.row_span(level):
                    at_level = level - plan.col_bits - 1
                    ex[level, k] = remote(
                        ex_out.at[at_level],
                        ex_in.at[at_level, k - 1],
                        ex_s.at[at_level, k - 1],
                        ex_r.at[at_level, k - 1],
                        row_peer(plan.row_span(level), k),
                    )
    first = remote(part.at[0], l1_in, l1_s.at[0], l1_r.at[0], col_peer(2, 1))
    sent += list(ex.values()) + [first]
    if plan.levels > plan.col_bits:
        low, high = plan.col_bits + 1, levels
        for level in range(low, high + 1):
            at_level = level - plan.col_bits - 1
            total = ex_out[at_level]
            for k in range(1, plan.row_span(level)):
                ex[level, k].wait_recv()
                total = total + ex_in[at_level, k - 1]
            final[level - 1, own_rows(level)] = total
            gather(level, level)
    sent += list(ag.values())

    def applied(low, high):
        coef = final[low - 1 : high].reshape(plan.sep * (high - low + 1), -1).astype(BF16)
        return jnp.dot(turned[:, plan.sep * (low - 1) : plan.sep * high], coef, preferred_element_type=F32)

    first.wait_recv()
    final[0] = part[0] + l1_in[...]
    for (low, m), copy in ag.items():
        if low <= plan.col_bits:
            copy.wait_recv()
    out_ref[...] += applied(1, plan.col_bits)
    for (low, m), copy in ag.items():
        if low > plan.col_bits:
            copy.wait_recv()
    out_ref[...] += applied(plan.col_bits + 1, levels)
    for copy in sent:
        copy.wait_send()


def in_one_kernel(plan, elem_residual, corners, share_rows, x_factor):
    rows_dev, cols = x_factor.shape
    shared = share_rows.shape[2]
    elems, kinds, width = elem_residual.shape
    levels, sep = plan.levels, plan.sep
    slots = plan.n_col - 1
    row_levels = levels - plan.col_bits
    row_slots = plan.n_row - 1
    half = sep // 4
    small = sep // plan.n_col
    dma = pltpu.SemaphoreType.DMA
    anywhere = pl.BlockSpec(memory_space=pl.ANY)
    return pl.pallas_call(
        functools.partial(kernel, plan),
        out_shape=pltpu.VMEM((rows_dev, width), F32),
        in_specs=[anywhere] * 4,
        out_specs=pl.BlockSpec(memory_space=pltpu.VMEM),
        scratch_shapes=[
            pltpu.VMEM((kinds, elems, width), BF16),
            pltpu.VMEM((kinds, elems), jnp.int32),
            pltpu.VMEM((2, shared), jnp.int32),
            pltpu.VMEM((cols, rows_dev), BF16),
            pltpu.VMEM((2, shared, width), F32),
            pltpu.VMEM((2, shared, width), F32),
            pltpu.VMEM((rows_dev, width), F32),
            pltpu.VMEM((rows_dev, width), BF16),
            pltpu.VMEM((levels, sep, width), F32),
            pltpu.VMEM((sep, width), F32),
            pltpu.VMEM((slots, levels, half, width), F32),
            pltpu.VMEM((row_levels, small, width), F32),
            pltpu.VMEM((row_levels, row_slots, small, width), F32),
            pltpu.VMEM((levels, sep, width), F32),
            pltpu.VMEM((rows_dev, sep * levels), BF16),
            dma((4,)),
            dma((2,)),
            dma((2,)),
            dma((1,)),
            dma((1,)),
            dma((levels, slots)),
            dma((levels, slots)),
            dma((row_levels, row_slots)),
            dma((row_levels, row_slots)),
            dma((levels, slots)),
            dma((levels, slots)),
        ],
        compiler_params=pltpu.CompilerParams(collective_id=0, has_side_effects=True),
        name="factor_solve",
    )(
        elem_residual.transpose(1, 0, 2),
        corners.T,
        share_rows.reshape(2, shared),
        x_factor.T,
    )


def solution(mesh):
    n_row, n_col = mesh.shape["row"], mesh.shape["col"]
    levels = (n_row * n_col).bit_length() - 1

    def per_device(elem_residual, corners, share_rows, x_factor):
        sep = (x_factor.shape[1] - INNER) // levels
        args = (elem_residual, corners, share_rows, x_factor)
        if takes(n_row, n_col, sep):
            return in_one_kernel(Plan(n_row, n_col, sep), *args)
        return by_rounds(n_row, n_col, *args)

    placed = (
        P(("row", "col"), None, None),
        P(("row", "col"), None),
        P(("row", "col"), None, None),
        P(("row", "col"), None),
    )
    return jax.shard_map(
        per_device, mesh=mesh, in_specs=placed, out_specs=P(("row", "col"), None), check_vma=False
    )
```

```python
import functools

import jax
import jax.numpy as jnp
from jax import lax
from jax.experimental import pallas as pl
from jax.experimental.pallas import tpu as pltpu
from jax.sharding import PartitionSpec as P

INNER = 1408
MESH = pl.DeviceIdType.MESH
F32 = jnp.float32
BF16 = jnp.bfloat16


def swapped(block, axis, stride):
    count = lax.axis_size(axis)
    route = []
    for low in range(count):
        high = low | 1 << stride
        if high != low and high < count:
            route += [(low, high), (high, low)]
    return lax.ppermute(block, axis, route)


def summed_levels(blocks, n_row, n_col):
    col_bits = n_col.bit_length() - 1
    row_bits = n_row.bit_length() - 1
    for bit in range(col_bits + row_bits):
        axis, stride = ("col", bit) if bit < col_bits else ("row", bit - col_bits)
        partner = swapped(blocks[bit:], axis, stride)
        blocks = jnp.concatenate([blocks[:bit], blocks[bit:] + partner], axis=0)
    return blocks


def by_rounds(n_row, n_col, elem_residual, corners, share_rows, x_factor):
    rows_dev = x_factor.shape[0]
    shared = share_rows.shape[2]
    width = elem_residual.shape[2]
    levels = (n_row * n_col).bit_length() - 1
    ext_len = rows_dev + 2 * shared
    flat_ids = corners.reshape(-1)
    onehot = (
        lax.broadcasted_iota(jnp.int32, (ext_len, flat_ids.shape[0]), 0) == flat_ids[None, :]
    ).astype(BF16)
    extended = jnp.dot(onehot, elem_residual.reshape(-1, width), preferred_element_type=F32)
    forward = [(i, (i + 1) % n_col) for i in range(n_col)]
    backward = [(target, source) for source, target in forward]
    from_left = lax.ppermute(extended[rows_dev + shared :], "col", forward)
    from_right = lax.ppermute(extended[rows_dev : rows_dev + shared], "col", backward)
    row_ids = lax.broadcasted_iota(jnp.int32, (rows_dev, shared), 0)
    assembled = extended[:rows_dev]
    for side, received in ((0, from_left), (1, from_right)):
        side_map = (row_ids == share_rows[0, side][None, :]).astype(F32)
        assembled = assembled + jnp.dot(
            side_map, received, precision=lax.Precision.HIGHEST, preferred_element_type=F32
        )
    partial_value = lax.dot_general(
        x_factor, assembled.astype(BF16), (((0,), (0,)), ((), ())), preferred_element_type=F32
    )
    blocks = partial_value[INNER:].reshape(levels, -1, width)
    blocks = summed_levels(blocks, n_row, n_col)
    coef = jnp.concatenate([partial_value[:INNER], blocks.reshape(-1, width)], axis=0)
    return jnp.dot(x_factor, coef.astype(BF16), preferred_element_type=F32)


class Plan:
    def __init__(self, n_row, n_col, sep):
        self.n_row, self.n_col, self.sep = n_row, n_col, sep
        self.levels = (n_row * n_col).bit_length() - 1
        self.col_bits = n_col.bit_length() - 1
        self.groups = []
        if self.levels > self.col_bits:
            self.groups += [(level, level) for level in range(self.levels, self.col_bits, -1)]
        self.groups += [(level, level) for level in range(self.col_bits, 1, -1)]

    def span(self, level):
        return min(2**level, self.n_col)

    def row_span(self, level):
        return max(1, 2**level // self.n_col)

    def piece(self, level):
        return self.sep // self.span(level)


def takes(n_row, n_col, sep):
    return n_col >= 4 and 2 <= n_row <= 4 and sep % (8 * n_col) == 0


def tdot(a, b):
    return lax.dot_general(a, b, (((0,), (0,)), ((), ())), preferred_element_type=F32)


def kernel(
    plan,
    er_hbm, cor_hbm, sh_hbm, x_hbm,
    out_ref,
    er, cor, sh, xt,
    halo_out, halo_in, own, rhs, part, l1_in, rs_in, ex_out, ex_in, final, turned,
    in_sem, halo_s, halo_r, l1_s, l1_r, rs_s, rs_r, ex_s, ex_r, ag_s, ag_r,
):
    row, col = lax.axis_index("row"), lax.axis_index("col")
    levels, n_col = plan.levels, plan.n_col
    rows_dev = out_ref.shape[0]
    shared = halo_out.shape[1]
    kinds = er.shape[0]
    elems = er.shape[1]
    inner = xt.shape[0] - plan.sep * levels

    right = (row, (col + 1) % n_col)
    left = (row, (col + n_col - 1) % n_col)

    def col_peer(span, m):
        local = col % span
        return (row, col - local + (local + m) % span)

    def row_peer(span, k):
        local = row % span
        return (row - local + (local + k) % span, col)

    greeted = [col_peer(n_col, m) for m in range(1, n_col)]
    greeted += [row_peer(plan.n_row, k) for k in range(1, plan.n_row)]
    barrier = pltpu.get_barrier_semaphore()
    for peer in greeted:
        pl.semaphore_signal(barrier, inc=1, device_id=peer, device_id_type=MESH)

    loads = [
        pltpu.make_async_copy(source, target, in_sem.at[i])
        for i, (source, target) in enumerate(
            ((cor_hbm, cor), (er_hbm, er), (sh_hbm, sh), (x_hbm, xt))
        )
    ]
    for load in loads:
        load.start()

    def assembled_rows(start, count):
        total = None
        for k in range(kinds):
            ids = cor[k : k + 1, :]
            at = lax.broadcasted_iota(jnp.int32, (count, elems), 0) + start
            onehot = jnp.where(at == ids, 1.0, 0.0).astype(BF16)
            term = jnp.dot(onehot, er[k], preferred_element_type=F32)
            total = term if total is None else total + term
        return total

    loads[0].wait()
    loads[1].wait()
    halo_out[...] = assembled_rows(rows_dev, 2 * shared).reshape(halo_out.shape)
    own[...] = assembled_rows(0, rows_dev)
    pl.semaphore_wait(barrier, len(greeted))

    def remote(source, target, send, recv, peer):
        copy = pltpu.make_async_remote_copy(
            src_ref=source,
            dst_ref=target,
            send_sem=send,
            recv_sem=recv,
            device_id=peer,
            device_id_type=MESH,
        )
        copy.start()
        return copy

    sent = []
    halo = [
        remote(halo_out.at[1], halo_in.at[0], halo_s.at[0], halo_r.at[0], right),
        remote(halo_out.at[0], halo_in.at[1], halo_s.at[1], halo_r.at[1], left),
    ]
    sent += halo

    loads[2].wait()
    targets = jnp.concatenate([sh[0:1, :], sh[1:2, :]], axis=1)
    at = lax.broadcasted_iota(jnp.int32, (rows_dev, 2 * shared), 0)
    share_map = jnp.where(at == targets, 1.0, 0.0).astype(BF16)
    share_map = jnp.concatenate([share_map, share_map], axis=1)
    loads[3].wait()
    for copy in halo:
        copy.wait_recv()
    received = halo_in[...].reshape(2 * shared, -1)
    high = received.astype(BF16)
    low = (received - high.astype(F32)).astype(BF16)
    received = jnp.concatenate([high, low], axis=0)
    assembled = own[...] + jnp.dot(share_map, received, preferred_element_type=F32)
    rhs[...] = assembled.astype(BF16)

    def partial(low, high):
        rows = xt[inner + plan.sep * (low - 1) : inner + plan.sep * high, :]
        block = jnp.dot(rows, rhs[...], preferred_element_type=F32)
        part[low - 1 : high] = block.reshape(high - low + 1, plan.sep, -1)


    def own_rows(level, ahead=0):
        span, rows = plan.span(level), plan.piece(level)
        return pl.ds(pl.multiple_of((col % span + ahead) % span * rows, 8), rows)

    rs, ex, ag = {}, {}, {}
    def scatter(low, high):
        count = high - low + 1
        for m in range(1, plan.span(low)):
            rs[low, m] = remote(
                part.at[pl.ds(low - 1, count), own_rows(low, m)],
                rs_in.at[m - 1, pl.ds(low - 1, count), pl.ds(0, plan.piece(low))],
                rs_s.at[low - 1, m - 1],
                rs_r.at[low - 1, m - 1],
                col_peer(plan.span(low), m),
            )
    partial(plan.col_bits + 1, levels)
    for group in plan.groups:
        if group[0] > plan.col_bits:
            scatter(*group)
    partial(1, plan.col_bits)
    weights = jnp.dot(xt[:inner, :], rhs[...], preferred_element_type=F32).astype(BF16)
    out_ref[...] = tdot(xt[:inner, :], weights)
    for group in plan.groups:
        if group[0] <= plan.col_bits:
            scatter(*group)
    first = remote(part.at[0], l1_in, l1_s.at[0], l1_r.at[0], col_peer(2, 1))
    turned[...] = xt[inner:, :].T
    sent += list(rs.values())

    def gather(low, high):
        count = high - low + 1
        block = final.at[pl.ds(low - 1, count), own_rows(low)]
        for m in range(1, plan.span(low)):
            ag[low, m] = remote(
                block,
                block,
                ag_s.at[low - 1, m - 1],
                ag_r.at[low - 1, m - 1],
                col_peer(plan.span(low), m),
            )

    for low, high in plan.groups:
        rows = plan.piece(low)
        for m in range(1, plan.span(low)):
            rs[low, m].wait_recv()
        for level in range(low, high + 1):
            total = part[level - 1, own_rows(level)]
            for m in range(1, plan.span(low)):
                total = total + rs_in[m - 1, level - 1, pl.ds(0, rows)]
            if level <= plan.col_bits:
                final[level - 1, own_rows(level)] = total
            else:
                ex_out[level - plan.col_bits - 1] = total
        if low <= plan.col_bits:
            gather(low, high)
            continue
        for k in range(plan.n_row - 1, 0, -1):
            for level in range(low, high + 1):
                if k < plan.row_span(level):
                    at_level = level - plan.col_bits - 1
                    ex[level, k] = remote(
                        ex_out.at[at_level],
                        ex_in.at[at_level, k - 1],
                        ex_s.at[at_level, k - 1],
                        ex_r.at[at_level, k - 1],
                        row_peer(plan.row_span(level), k),
                    )
    sent += list(ex.values()) + [first]
    if plan.levels > plan.col_bits:
        low, high = plan.col_bits + 1, levels
        for level in range(low, high + 1):
            at_level = level - plan.col_bits - 1
            total = ex_out[at_level]
            for k in range(1, plan.row_span(level)):
                ex[level, k].wait_recv()
                total = total + ex_in[at_level, k - 1]
            final[level - 1, own_rows(level)] = total
            gather(level, level)
    sent += list(ag.values())

    def applied(low, high):
        coef = final[low - 1 : high].reshape(plan.sep * (high - low + 1), -1).astype(BF16)
        return jnp.dot(turned[:, plan.sep * (low - 1) : plan.sep * high], coef, preferred_element_type=F32)

    first.wait_recv()
    final[0] = part[0] + l1_in[...]
    for (low, m), copy in ag.items():
        if low <= plan.col_bits:
            copy.wait_recv()
    out_ref[...] += applied(1, plan.col_bits)
    for (low, m), copy in ag.items():
        if low > plan.col_bits:
            copy.wait_recv()
    out_ref[...] += applied(plan.col_bits + 1, levels)
    for copy in sent:
        copy.wait_send()


def in_one_kernel(plan, elem_residual, corners, share_rows, x_factor):
    rows_dev, cols = x_factor.shape
    shared = share_rows.shape[2]
    elems, kinds, width = elem_residual.shape
    levels, sep = plan.levels, plan.sep
    slots = plan.n_col - 1
    row_levels = levels - plan.col_bits
    row_slots = plan.n_row - 1
    half = sep // 4
    small = sep // plan.n_col
    dma = pltpu.SemaphoreType.DMA
    anywhere = pl.BlockSpec(memory_space=pl.ANY)
    return pl.pallas_call(
        functools.partial(kernel, plan),
        out_shape=pltpu.VMEM((rows_dev, width), F32),
        in_specs=[anywhere] * 4,
        out_specs=pl.BlockSpec(memory_space=pltpu.VMEM),
        scratch_shapes=[
            pltpu.VMEM((kinds, elems, width), BF16),
            pltpu.VMEM((kinds, elems), jnp.int32),
            pltpu.VMEM((2, shared), jnp.int32),
            pltpu.VMEM((cols, rows_dev), BF16),
            pltpu.VMEM((2, shared, width), F32),
            pltpu.VMEM((2, shared, width), F32),
            pltpu.VMEM((rows_dev, width), F32),
            pltpu.VMEM((rows_dev, width), BF16),
            pltpu.VMEM((levels, sep, width), F32),
            pltpu.VMEM((sep, width), F32),
            pltpu.VMEM((slots, levels, half, width), F32),
            pltpu.VMEM((row_levels, small, width), F32),
            pltpu.VMEM((row_levels, row_slots, small, width), F32),
            pltpu.VMEM((levels, sep, width), F32),
            pltpu.VMEM((rows_dev, sep * levels), BF16),
            dma((4,)),
            dma((2,)),
            dma((2,)),
            dma((1,)),
            dma((1,)),
            dma((levels, slots)),
            dma((levels, slots)),
            dma((row_levels, row_slots)),
            dma((row_levels, row_slots)),
            dma((levels, slots)),
            dma((levels, slots)),
        ],
        compiler_params=pltpu.CompilerParams(collective_id=0, has_side_effects=True),
        name="factor_solve",
    )(
        elem_residual.transpose(1, 0, 2),
        corners.T,
        share_rows.reshape(2, shared),
        x_factor.T,
    )


def solution(mesh):
    n_row, n_col = mesh.shape["row"], mesh.shape["col"]
    levels = (n_row * n_col).bit_length() - 1

    def per_device(elem_residual, corners, share_rows, x_factor):
        sep = (x_factor.shape[1] - INNER) // levels
        args = (elem_residual, corners, share_rows, x_factor)
        if takes(n_row, n_col, sep):
            return in_one_kernel(Plan(n_row, n_col, sep), *args)
        return by_rounds(n_row, n_col, *args)

    placed = (
        P(("row", "col"), None, None),
        P(("row", "col"), None),
        P(("row", "col"), None, None),
        P(("row", "col"), None),
    )
    return jax.shard_map(
        per_device, mesh=mesh, in_specs=placed, out_specs=P(("row", "col"), None), check_vma=False
    )
```
